128 devices in a mesh: pipe: 4 (over z_hi, core), expert: 32 (over z_lo, y, x).
Axes of the slice: x: 4, y: 4, z: 4 (z_hi: 2, z_lo: 2; z = z_hi * 2 + z_lo), core: 2. Of those that a mesh axis runs over, the one named last changes fastest.
Arguments:
- tokens: bfloat16 [4, 4096, 2048], P('pipe', 'expert'), may hold values from -6 to 6
- expert_ids: int32 [4, 4096, 4], P('pipe', 'expert'), may hold values from 0 to 31, all different within a row; in each aligned block of 128 rows (0 to 127, 128 to 255, ..., all dimensions but the last counted through in order) at most 24 rows name the same one
- route_weights: float32 [4, 4096, 4], P('pipe', 'expert'), may hold values from 0.05 to 0.5
- out_grad: bfloat16 [4, 4096, 2048], P('pipe', 'expert'), may hold values from -1.5 to 1.5
- gate_proj: bfloat16 [2, 32, 2048, 768], P(None, 'expert'), may hold values from -0.125 to 0.125
- up_proj: bfloat16 [2, 32, 2048, 768], P(None, 'expert'), may hold values from -0.125 to 0.125
- down_proj: bfloat16 [2, 32, 768, 2048], P(None, 'expert'), may hold values from -0.21875 to 0.21875
Outputs:
- layer_out: bfloat16 [4, 4096, 2048], P('pipe', 'expert')
- input_grad: bfloat16 [4, 4096, 2048], P('pipe', 'expert')
- gate_grad: float32 [4, 4096, 4], P('pipe', 'expert')
- grad_gate_proj: bfloat16 [4, 32, 2048, 384], P('pipe', 'expert')
- grad_up_proj: bfloat16 [4, 32, 2048, 384], P('pipe', 'expert')
- grad_down_proj: bfloat16 [4, 32, 384, 2048], P('pipe', 'expert')
The draws below stay inside these ranges and needn't reach their ends.
Inputs may be any that keep to these rules, and one draw needn't show every extreme that they name: `expert_ids`: A token's 4 experts differ. Among the pairs of one device's 128 tokens no expert is named more than 24 times, a bound that some block reaches.
All inputs are finite; a program needn't handle non-finite values.
Results may differ from the reference program's by a relative error of at most 0.0066.
Values may be sent and summed in bfloat16 or wider, within the bound.
No kernel may reach another device: no remote copies, remote signals or barrier semaphores. Data moves between devices by JAX's collectives and lax.ppermute only.
A program may use at most 128 MiB of HBM per device.

```python
import math
import jax
import jax.numpy as jnp
import numpy as np

D = 2048
FF = 768
HALF = 384
TOK_DEV = 128
TOPK = 4
EXPERTS = 32
SLOTS = 24
TOKENS = 4096
PAIRS = 2
N_PIPE = 4
N_EXPERT = 32


def block_levels(own_key, extent, split, low, largest):
    factor_of = 1.0
    for dim, parts in split:
        heights = jax.random.uniform(jax.random.fold_in(jax.random.fold_in(own_key, 6), dim), (parts,), jnp.float32, low / len(split), largest / len(split))
        factor_of = factor_of * jnp.repeat(jnp.exp(heights), extent[dim] // parts).reshape((-1,) + (1,) * (len(extent) - 1 - dim))
    return factor_of


def shared_out(own_key, own, number, rows, count, top, reach, skew):
    order = jax.random.permutation(own_key, count)
    packed, usual = shares(count, rows * top, reach, skew, True), shares(count, rows * top, reach, skew, False)
    places = jnp.arange(count)

    def named(tallies, rotation):
        used = int((tallies > 0).sum())
        fixed = max(1, used // 4)
        moved = fixed + (places - fixed + rotation * (used - fixed)) % max(1, count - fixed)
        return jnp.zeros((count,), jnp.int32).at[order[jnp.where(places < fixed, places, moved)]].set(jnp.asarray(tallies, jnp.int32))

    tallies = jnp.where(number % 4 == 0, named(packed, number // 4), named(usual, number - number // 4 - 1))
    mixed = jax.random.permutation(jax.random.fold_in(own, 3), count)
    giver, receiver = mixed[0:count // 2 * 2:2], mixed[1:count // 2 * 2:2]
    slack = jnp.minimum(tallies[giver] - 1, reach - tallies[receiver]) // 2
    slack = jnp.where((giver == order[0]) | (receiver == order[0]) | (tallies[receiver] == 0), 0, jnp.maximum(slack, 0))
    moved = jax.random.randint(jax.random.fold_in(own, 4), (count // 2,), 0, 1 << 20) % (slack + 1)
    tallies = tallies.at[giver].add(-moved).at[receiver].add(moved)
    items = jnp.searchsorted(jnp.cumsum(tallies), jnp.arange(rows * top), side="right").astype(jnp.int32)
    grid = items.reshape(top, rows).T
    grid = grid[jax.random.permutation(jax.random.fold_in(own, 1), rows)]
    rotation = jax.random.randint(jax.random.fold_in(own, 2), (rows, 1), 0, top)
    return jnp.take_along_axis(grid, (jnp.arange(top)[None, :] + rotation) % top, axis=1)


def shares(number_of, total, limit, skew, full):
    weights = [(1 << 20) // math.isqrt(rank ** skew) + 1 for rank in range(1, number_of + 1)]
    largest = limit if full else min(limit, max(-(-total // number_of), total * weights[0] // sum(weights)))
    least = 1 if total - largest >= number_of - 1 else 0
    given, rest = [largest] + [least] * (number_of - 1), total - largest - least * (number_of - 1)
    while rest > 0:
        free = [i for i in range(1, number_of) if given[i] < largest] or [i for i in range(1, number_of) if given[i] < limit]
        pool, remaining = sum([weights[i] for i in free]), rest
        for i in free:
            more = min(limit - given[i], max(1, remaining * weights[i] // pool), rest)
            given[i] = given[i] + more
            rest = rest - more
    return np.array(given)


def gaussian(key, extent, scale, most, shards=(), held_as=jnp.bfloat16):
    result = jax.random.normal(key, extent, jnp.float32) * scale
    if len(shards) > 0:
        result = block_levels(key, extent, shards, -0.22, 0.18) * result
    return jnp.clip(result, min=-most, max=most).astype(held_as)


def setup_inputs(seed: int = 0) -> dict:
    keys = jax.random.split(jax.random.key(seed), 8)
    tokens = gaussian(keys[0], (N_PIPE, TOKENS, D), 1.0, 6.0, ((0, 4), (1, 32)))
    expert_ids_keys = jax.random.split(jax.random.fold_in(keys[1], 1), N_PIPE * TOKENS // TOK_DEV)
    expert_ids_turns = jax.random.permutation(jax.random.fold_in(keys[1], 3), N_PIPE * TOKENS // TOK_DEV)
    expert_ids = jax.vmap(lambda own, number: shared_out(jax.random.fold_in(keys[1], 2), own, number, TOK_DEV, EXPERTS, TOPK, SLOTS, 1))(expert_ids_keys, expert_ids_turns).reshape((N_PIPE, TOKENS, TOPK))
    route_weights = jnp.clip(jnp.exp(math.log(0.5) - 2.3025851 * jax.random.uniform(keys[2], (N_PIPE, TOKENS, TOPK), jnp.float32) ** block_levels(keys[2], (N_PIPE, TOKENS, TOPK), ((0, 4), (1, 32)), -0.2, 0.2)), 0.05, 0.5)
    out_grad = gaussian(keys[3], (N_PIPE, TOKENS, D), 0.25, 1.5, ((0, 4), (1, 32)))
    gate_proj = gaussian(keys[4], (PAIRS, EXPERTS, D, FF), D ** -0.5, 0.125, ((1, 32),))
    up_proj = gaussian(keys[5], (PAIRS, EXPERTS, D, FF), D ** -0.5, 0.125, ((1, 32),))
    down_proj = gaussian(keys[6], (PAIRS, EXPERTS, FF, D), FF ** -0.5, 0.21875, ((1, 32),))
    return {"tokens": tokens, "expert_ids": expert_ids, "route_weights": route_weights, "out_grad": out_grad, "gate_proj": gate_proj, "up_proj": up_proj, "down_proj": down_proj}


def slot_positions(routed, experts, slot_count):
    table = (routed[:, None] == jnp.arange(experts, dtype=jnp.int32)[None, :]).astype(jnp.int32)
    earlier = jnp.cumsum(table, axis=0) - table
    within = jnp.sum(earlier * table, axis=1)
    return (routed * slot_count + within).astype(jnp.int32)


def inverse_map(positions, total_slots, sentinel):
    filler = jnp.full((total_slots,), sentinel, jnp.int32)
    return filler.at[positions].set(jnp.arange(positions.shape[0], dtype=jnp.int32))


def take_rows(source, index):
    return jax.vmap(lambda block_rows, block_index: block_rows[block_index])(source, index)


def to_expert(source):
    width_last = source.shape[-1]
    return source.reshape(N_EXPERT, EXPERTS, SLOTS, width_last).transpose(1, 0, 2, 3).reshape(EXPERTS, N_EXPERT * SLOTS, width_last)


def from_expert(source):
    width_last = source.shape[-1]
    return source.reshape(EXPERTS, N_EXPERT, SLOTS, width_last).transpose(1, 0, 2, 3).reshape(N_EXPERT, EXPERTS * SLOTS, width_last)


def reference(tokens, expert_ids, route_weights, out_grad, gate_proj, up_proj, down_proj):
    pair_count = TOK_DEV * TOPK
    row_total = EXPERTS * SLOTS
    layer_outs = []
    input_grads = []
    gate_grads = []
    section_grads = []
    for section_index in range(N_PIPE):
        layer_index = min(section_index, N_PIPE - 1 - section_index)
        w_gate = gate_proj[layer_index].astype(jnp.float32)
        w_up = up_proj[layer_index].astype(jnp.float32)
        w_down = down_proj[layer_index].astype(jnp.float32)
        routed = expert_ids[section_index].reshape(N_EXPERT, pair_count)
        positions = jax.vmap(lambda block_ids: slot_positions(block_ids, EXPERTS, SLOTS))(routed)
        inverse = jax.vmap(lambda block_pos: inverse_map(block_pos, row_total, pair_count))(positions)
        local_rows = tokens[section_index].reshape(N_EXPERT, TOK_DEV, D)
        padded = jnp.concatenate([local_rows, jnp.zeros((N_EXPERT, 1, D), jnp.bfloat16)], axis=1)
        expert_rows = to_expert(take_rows(padded, inverse // TOPK)).astype(jnp.float32)
        gate_pre = jnp.einsum("erd,edf->erf", expert_rows, w_gate)
        up_pre = jnp.einsum("erd,edf->erf", expert_rows, w_up)
        hidden = (jax.nn.silu(gate_pre) * up_pre).astype(jnp.bfloat16)
        expert_out = jnp.einsum("erf,efd->erd", hidden.astype(jnp.float32), w_down).astype(jnp.bfloat16)
        pair_out = take_rows(from_expert(expert_out), positions).reshape(TOKENS, TOPK, D).astype(jnp.float32)
        mixing = route_weights[section_index]
        layer_outs.append(jnp.sum(mixing[:, :, None] * pair_out, axis=1).astype(jnp.bfloat16))
        cotangent = out_grad[section_index].astype(jnp.float32)
        gate_grads.append(jnp.sum(cotangent[:, None, :] * pair_out, axis=2))
        weighted_grad = (mixing[:, :, None] * cotangent[:, None, :]).astype(jnp.bfloat16).reshape(N_EXPERT, pair_count, D)
        padded_grad = jnp.concatenate([weighted_grad, jnp.zeros((N_EXPERT, 1, D), jnp.bfloat16)], axis=1)
        grad_rows = to_expert(take_rows(padded_grad, inverse)).astype(jnp.float32)
        hidden_grad = jnp.einsum("erd,efd->erf", grad_rows, w_down)
        sigmoid_gate = jax.nn.sigmoid(gate_pre)
        gate_pre_grad = (hidden_grad * up_pre * sigmoid_gate * (1.0 + gate_pre * (1.0 - sigmoid_gate))).astype(jnp.bfloat16).astype(jnp.float32)
        up_pre_grad = (hidden_grad * gate_pre * sigmoid_gate).astype(jnp.bfloat16).astype(jnp.float32)
        row_input_grad = (jnp.einsum("erf,edf->erd", gate_pre_grad, w_gate) + jnp.einsum("erf,edf->erd", up_pre_grad, w_up)).astype(jnp.bfloat16)
        pair_grad = take_rows(from_expert(row_input_grad), positions).reshape(TOKENS, TOPK, D).astype(jnp.float32)
        input_grads.append(jnp.sum(pair_grad, axis=1).astype(jnp.bfloat16))
        grad_gate = jnp.einsum("erd,erf->edf", expert_rows, gate_pre_grad).astype(jnp.bfloat16)
        grad_up = jnp.einsum("erd,erf->edf", expert_rows, up_pre_grad).astype(jnp.bfloat16)
        grad_down = jnp.einsum("erf,erd->efd", hidden.astype(jnp.float32), grad_rows).astype(jnp.bfloat16)
        section_grads.append((grad_gate, grad_up, grad_down))
    kept_gate = []
    kept_up = []
    kept_down = []
    for section_index in range(N_PIPE):
        mirror_index = N_PIPE - 1 - section_index
        start = HALF if section_index >= N_PIPE // 2 else 0
        summed = [(section_grads[section_index][slot_kind].astype(jnp.float32) + section_grads[mirror_index][slot_kind].astype(jnp.float32)).astype(jnp.bfloat16) for slot_kind in range(3)]
        kept_gate.append(summed[0][:, :, start:start + HALF])
        kept_up.append(summed[1][:, :, start:start + HALF])
        kept_down.append(summed[2][:, start:start + HALF, :])
    return (jnp.stack(layer_outs), jnp.stack(input_grads), jnp.stack(gate_grads), jnp.stack(kept_gate), jnp.stack(kept_up), jnp.stack(kept_down))
```

```python
import functools

import jax
import jax.numpy as jnp
from jax import lax
from jax.experimental import pallas as pl
from jax.experimental.pallas import tpu as pltpu
from jax.sharding import Mesh, PartitionSpec as P

AXES = ("zh", "c", "zl", "y", "x")
EXPERT = ("zl", "y", "x")
SIZES = (2, 2, 2, 4, 4)
VMEM_LIMIT = 48 << 20


def pairs(fn):
    out = []
    for i in range(128):
        zh, c, zl, yx = i >> 6, i >> 5 & 1, i >> 4 & 1, i & 15
        zh, c, zl = fn(zh, c, zl)
        out.append((i, (zh << 6) | (c << 5) | (zl << 4) | yx))
    return out


SWAP = [(i, j) for i, j in pairs(lambda zh, c, zl: (zh ^ c, c, zl)) if i != j]
SIBLING = pairs(lambda zh, c, zl: (zh, c ^ 1, zl))


def move(value, table):
    return lax.ppermute(value, AXES, table)


def dot(a, b, ca, cb):
    return lax.dot_general(a, b, (((ca,), (cb,)), ((), ())), preferred_element_type=jnp.float32)


def vmem(count):
    return [pl.BlockSpec(memory_space=pltpu.VMEM)] * count


def call(kernel, out_shape, smem_args, args, flops, name):
    in_specs = [pl.BlockSpec(memory_space=pltpu.SMEM)] * len(smem_args) + vmem(len(args))
    single = not isinstance(out_shape, (tuple, list))
    shapes = [out_shape] if single else list(out_shape)
    moved = sum(a.size * a.dtype.itemsize for a in args) + sum(s.size * s.dtype.itemsize for s in shapes)
    return pl.pallas_call(
        kernel,
        out_shape=out_shape,
        in_specs=in_specs,
        out_specs=vmem(1)[0] if single else vmem(len(shapes)),
        compiler_params=pltpu.CompilerParams(vmem_limit_bytes=VMEM_LIMIT),
        cost_estimate=pl.CostEstimate(flops=flops, bytes_accessed=moved, transcendentals=0),
        name=name,
    )(*smem_args, *args)


def route_kernel(core_ref, own_ref, other_ref, meta_ref, s_ref, h_ref, l_ref):
    meta = jnp.where(core_ref[0] == 0, own_ref[...], other_ref[...])
    meta_ref[...] = meta
    expert = lax.broadcasted_iota(jnp.int32, (32, 128), 0).astype(jnp.float32)
    before = (
        lax.broadcasted_iota(jnp.int32, (128, 128), 0) < lax.broadcasted_iota(jnp.int32, (128, 128), 1)
    ).astype(jnp.bfloat16)
    row_e = lax.broadcasted_iota(jnp.int32, (768, 32), 0) // 24
    spread = (row_e == lax.broadcasted_iota(jnp.int32, (768, 32), 1)).astype(jnp.bfloat16)
    slot = (lax.broadcasted_iota(jnp.int32, (768, 128), 0) % 24).astype(jnp.float32)
    named = jnp.zeros((32, 128), jnp.float32)
    weight = jnp.zeros((32, 128), jnp.float32)
    for k in range(4):
        hit = (meta[k : k + 1, :] == expert).astype(jnp.float32)
        named = named + hit
        weight = weight + hit * meta[4 + k : 5 + k, :]
    earlier = dot(named.astype(jnp.bfloat16), before, 1, 0)
    place = jnp.where(named > 0.5, earlier, -1.0).astype(jnp.bfloat16)
    hit = dot(spread, place, 1, 0) == slot
    high = weight.astype(jnp.bfloat16)
    low = (weight - high.astype(jnp.float32)).astype(jnp.bfloat16)
    s_ref[...] = hit.astype(jnp.float32).astype(jnp.bfloat16)
    h_ref[...] = jnp.where(hit, dot(spread, high, 1, 0), 0.0).astype(jnp.bfloat16)
    l_ref[...] = jnp.where(hit, dot(spread, low, 1, 0), 0.0).astype(jnp.bfloat16)


def pick_kernel(core_ref, s_ref, own_ref, other_ref, o_ref):
    block = jnp.where(core_ref[0] == 0, own_ref[...], other_ref[...])
    o_ref[...] = dot(s_ref[...], block, 1, 0).astype(jnp.bfloat16)


def pick_weighted_kernel(core_ref, h_ref, l_ref, own_ref, other_ref, o_ref, block_ref):
    block = jnp.where(core_ref[0] == 0, own_ref[...], other_ref[...])
    block_ref[...] = block
    o_ref[...] = (dot(h_ref[...], block, 1, 0) + dot(l_ref[...], block, 1, 0)).astype(jnp.bfloat16)


def combine_kernel(meta_ref, s_ref, h_ref, l_ref, g_ref, r_ref, p_ref, t_ref):
    rows = r_ref[...]
    expert = lax.broadcasted_iota(jnp.int32, (32, 128), 0).astype(jnp.float32)
    p_ref[...] = (dot(h_ref[...], rows, 0, 0) + dot(l_ref[...], rows, 0, 0)).astype(jnp.bfloat16)
    kept = jnp.where(s_ref[...] > 0.5, dot(rows, g_ref[...], 1, 1), 0.0)
    by_expert = jnp.sum(kept.reshape(32, 24, 128), axis=1)
    for k in range(4):
        hit = meta_ref[k : k + 1, :] == expert
        t_ref[k : k + 1, :] = jnp.sum(jnp.where(hit, by_expert, 0.0), axis=0, keepdims=True)
    t_ref[4:8, :] = jnp.zeros((4, 128), jnp.float32)


def gather_sum_kernel(s_ref, r_ref, p_ref):
    p_ref[...] = dot(s_ref[...], r_ref[...], 0, 0).astype(jnp.bfloat16)


def exchange(rows):
    return lax.all_to_all(rows.reshape(32, 24, 2048), EXPERT, 0, 0, tiled=True).reshape(768, 2048)


def shards(tokens, expert_ids, route_weights, out_grad, gate_proj, up_proj, down_proj):
    f32, bf16 = jnp.float32, jnp.bfloat16
    sds = jax.ShapeDtypeStruct
    zh = lax.axis_index("zh")
    core = lax.axis_index("c")
    core_arg = core.reshape(1)
    meta = jnp.concatenate([expert_ids[0].T.astype(f32), route_weights[0].T], axis=0)

    select = sds((768, 128), bf16)
    rows_shape = sds((768, 2048), bf16)
    block_shape = sds((128, 2048), bf16)
    tiny = sds((8, 128), f32)
    meta, pick, high, low = call(
        route_kernel, (tiny, select, select, select), [core_arg], [meta, move(meta, SWAP)], 30_000_000, "route"
    )
    tok = tokens[0]
    rows = call(pick_kernel, rows_shape, [core_arg], [pick, tok, move(tok, SWAP)], 400_000_000, "pick_tokens")
    rows = exchange(rows)
    grads, og = call(
        pick_weighted_kernel,
        (rows_shape, block_shape),
        [core_arg],
        [high, low, out_grad[0], move(out_grad[0], SWAP)],
        800_000_000,
        "pick_grads",
    )
    grads = exchange(grads)

    w_gate = lax.dynamic_index_in_dim(gate_proj, zh, 0, keepdims=False)[0]
    w_up = lax.dynamic_index_in_dim(up_proj, zh, 0, keepdims=False)[0]
    w_down = lax.dynamic_index_in_dim(down_proj, zh, 0, keepdims=False)[0]
    gate_pre = dot(rows, w_gate, 1, 0)
    up_pre = dot(rows, w_up, 1, 0)
    sig = jax.nn.sigmoid(gate_pre)
    hidden = (gate_pre * sig * up_pre).astype(bf16)
    expert_out = dot(hidden, w_down, 1, 0).astype(bf16)
    returned = exchange(expert_out)
    part, gate_grad = call(
        combine_kernel, (block_shape, tiny), [], [meta, pick, high, low, og, returned], 1_200_000_000, "combine"
    )

    def home(value):
        return jnp.where(core == 0, value, move(value, SWAP))

    layer_out = home(part)
    gate_grad = home(gate_grad)[:4].T

    hidden_grad = dot(grads, w_down, 1, 1)
    d_gate = (hidden_grad * up_pre * sig * (1.0 + gate_pre * (1.0 - sig))).astype(bf16)
    d_up = (hidden_grad * gate_pre * sig).astype(bf16)

    mine = jnp.where(core == 0, zh, 1 - zh) * 384

    def weight_grads(start):
        cut = lambda v: lax.dynamic_slice_in_dim(v, start, 384, 1)
        both = jnp.concatenate([cut(d_gate), cut(d_up)], axis=1)
        return dot(rows, both, 0, 0).astype(bf16), dot(cut(hidden), grads, 0, 0).astype(bf16)

    theirs = [move(v, SIBLING) for v in weight_grads(384 - mine)]
    kept = weight_grads(mine)
    summed = [(a.astype(f32) + b.astype(f32)).astype(bf16) for a, b in zip(kept, theirs)]
    both, down = [home(v) for v in summed]

    row_grad = (dot(d_gate, w_gate, 1, 1) + dot(d_up, w_up, 1, 1)).astype(bf16)
    row_grad = exchange(row_grad)
    input_grad = home(call(gather_sum_kernel, block_shape, [], [pick, row_grad], 400_000_000, "gather_sum"))
    return (
        layer_out[None],
        input_grad[None],
        gate_grad[None],
        both[None, None, :, :384],
        both[None, None, :, 384:],
        down[None, None],
    )


def solution(mesh):
    fine = Mesh(mesh.devices.reshape(SIZES), AXES)
    pipe, expert = ("zh", "c"), ("zl", "y", "x")
    tok = P(pipe, expert, None)
    weight = P(None, expert, None, None)
    grad = P(pipe, expert, None, None)
    return jax.shard_map(
        shards,
        mesh=fine,
        in_specs=(tok, tok, tok, tok, weight, weight, weight),
        out_specs=(tok, tok, tok, grad, grad, grad),
        check_vma=False,
    )
```

```python
import functools

import jax
import jax.numpy as jnp
from jax import lax
from jax.experimental import pallas as pl
from jax.experimental.pallas import tpu as pltpu
from jax.sharding import Mesh, PartitionSpec as P


AXES = ("zh", "c", "zl", "y", "x")
SOURCE = ("zl", "y", "x")
SIZES = (2, 2, 2, 4, 4)
VMEM_LIMIT = 48 << 20


def pairs(fn):
    out = []
    for i in range(128):
        zh, c, zl, yx = i >> 6, i >> 5 & 1, i >> 4 & 1, i & 15
        zh, c, zl = fn(zh, c, zl)
        out.append((i, (zh << 6) | (c << 5) | (zl << 4) | yx))
    return out


def plane(dy, dx):
    def target(i):
        return i & ~15 | ((i >> 2) + dy & 3) << 2 | (i + dx & 3)

    return [(i, target(i)) for i in range(128)]


SWAP = [(i, j) for i, j in pairs(lambda zh, c, zl: (zh ^ c, c, zl)) if i != j]
CROSS = pairs(lambda zh, c, zl: (zh ^ c, c, zl ^ 1))
SIBLING = pairs(lambda zh, c, zl: (zh, c ^ 1, zl))


def move(value, table):
    return lax.ppermute(value, AXES, table)


def dot(a, b, ca, cb):
    return lax.dot_general(a, b, (((ca,), (cb,)), ((), ())), preferred_element_type=jnp.float32)


def vmem(count):
    return [pl.BlockSpec(memory_space=pltpu.VMEM)] * count


def call(kernel, out_shape, smem_args, args, flops, scratch=()):
    in_specs = [pl.BlockSpec(memory_space=pltpu.SMEM)] * len(smem_args) + vmem(len(args))
    single = not isinstance(out_shape, (tuple, list))
    shapes = [out_shape] if single else list(out_shape)
    moved = sum(a.size * a.dtype.itemsize for a in args) + sum(s.size * s.dtype.itemsize for s in shapes)
    return pl.pallas_call(
        kernel,
        out_shape=out_shape,
        in_specs=in_specs,
        out_specs=vmem(1)[0] if single else vmem(len(shapes)),
        scratch_shapes=scratch,
        compiler_params=pltpu.CompilerParams(vmem_limit_bytes=VMEM_LIMIT),
        cost_estimate=pl.CostEstimate(flops=flops, bytes_accessed=moved, transcendentals=0),
    )(*smem_args, *args)


def places(meta):
    expert = lax.broadcasted_iota(jnp.int32, (32, 128), 0).astype(jnp.float32)
    before = (
        lax.broadcasted_iota(jnp.int32, (128, 128), 0) < lax.broadcasted_iota(jnp.int32, (128, 128), 1)
    ).astype(jnp.bfloat16)
    named = jnp.zeros((32, 128), jnp.float32)
    weight = jnp.zeros((32, 128), jnp.float32)
    for k in range(4):
        hit = (meta[k : k + 1, :] == expert).astype(jnp.float32)
        named = named + hit
        weight = weight + hit * meta[4 + k : 5 + k, :]
    earlier = dot(named.astype(jnp.bfloat16), before, 1, 0)
    place = jnp.where(named > 0.5, earlier, -1.0).astype(jnp.bfloat16)
    high = weight.astype(jnp.bfloat16)
    low = (weight - high.astype(jnp.float32)).astype(jnp.bfloat16)
    return place, high, low


def selection(row_expert, slot, kept, place, high, low):
    spread = (row_expert == lax.broadcasted_iota(jnp.int32, (768, 32), 1)).astype(jnp.bfloat16)
    hit = dot(spread, place, 1, 0) == slot
    if kept is not None:
        hit = hit & kept
    pick = hit.astype(jnp.float32).astype(jnp.bfloat16)
    if high is None:
        return pick
    return (
        pick,
        jnp.where(hit, dot(spread, high, 1, 0), 0.0).astype(jnp.bfloat16),
        jnp.where(hit, dot(spread, low, 1, 0), 0.0).astype(jnp.bfloat16),
    )


def row_slot():
    return (lax.broadcasted_iota(jnp.int32, (768, 128), 0) % 24).astype(jnp.float32)


def route_kernel(at_ref, own_ref, other_ref, meta_ref, s_ref, h_ref, l_ref):
    meta = jnp.where(at_ref[1] == 0, own_ref[...], other_ref[...])
    meta_ref[...] = meta
    place, high, low = places(meta)
    row_expert = lax.broadcasted_iota(jnp.int32, (768, 32), 0) // 24
    s_ref[...], h_ref[...], l_ref[...] = selection(row_expert, row_slot(), None, place, high, low)


def plane_expert(at_ref, shape, x_first):
    group = lax.broadcasted_iota(jnp.int32, shape, 0) // 48
    dx, dy = (group // 4, group % 4) if x_first else (group % 4, group // 4)
    return at_ref[2] * 16 + (at_ref[3] + dy) % 4 * 4 + (at_ref[4] + dx) % 4


def back_route_kernel(at_ref, mine_ref, near_ref, s_ref, h_ref, l_ref, in_ref):
    slot = row_slot()
    half = lax.broadcasted_iota(jnp.int32, (768, 128), 0) % 48 // 24
    expert = plane_expert(at_ref, (768, 32), True)
    in_expert = plane_expert(at_ref, (768, 32), False)
    for b, ref in enumerate((mine_ref, near_ref)):
        place, high, low = places(ref[...])
        kept = half == jnp.where(at_ref[2] == 0, b, 1 - b)
        lanes = pl.ds(128 * b, 128)
        s_ref[:, lanes], h_ref[:, lanes], l_ref[:, lanes] = selection(expert, slot, kept, place, high, low)
        in_ref[:, lanes] = selection(in_expert, slot, kept, place, None, None)


def over_columns(count, width, body):
    @pl.loop(0, count)
    def _(i):
        body(pl.ds(pl.multiple_of(i * width, 128), width))


def pick_kernel(at_ref, s_ref, own_ref, other_ref, o_ref):
    def part(c):
        block = jnp.where(at_ref[1] == 0, own_ref[:, c], other_ref[:, c])
        o_ref[:, c] = dot(s_ref[...], block, 1, 0).astype(jnp.bfloat16)

    over_columns(4, 512, part)


def pick_weighted_kernel(at_ref, h_ref, l_ref, own_ref, other_ref, o_ref, block_ref):
    def part(c):
        block = jnp.where(at_ref[1] == 0, own_ref[:, c], other_ref[:, c])
        block_ref[:, c] = block
        o_ref[:, c] = (dot(h_ref[...], block, 1, 0) + dot(l_ref[...], block, 1, 0)).astype(jnp.bfloat16)

    over_columns(4, 512, part)


def down_kernel(at_ref, h_ref, w_ref, *o_refs):
    weight = w_ref[0, 0]
    for d, o_ref in enumerate(o_refs):
        start = pl.multiple_of((at_ref[3] + 4 - d) % 4 * 192, 16)
        o_ref[...] = dot(h_ref[pl.ds(start, 192), :], weight, 1, 0).astype(jnp.bfloat16)


def row_kernel(at_ref, g_ref, u_ref, wg_ref, wu_ref, *o_refs):
    w_gate = wg_ref[...]
    w_up = wu_ref[...]
    for d, o_ref in enumerate(o_refs):
        x = (at_ref[4] + 4 - d) % 4
        take = lambda ref: jnp.concatenate(
            [ref[pl.ds(pl.multiple_of(192 * y + 48 * x, 16), 48), :] for y in range(4)], axis=0
        )
        o_ref[...] = (dot(take(g_ref), w_gate, 1, 0) + dot(take(u_ref), w_up, 1, 0)).astype(jnp.bfloat16)


def turn_kernel(at_ref, a_ref, b_ref, ta_ref, tb_ref):
    ta_ref[...] = a_ref[0, 0].T
    tb_ref[...] = b_ref[0, 0].T


def regroup_kernel(axis, at_ref, *refs):
    for d in range(4):
        start = pl.multiple_of((at_ref[axis] + 4 - d) % 4 * 48, 16)
        for j in range(4):
            refs[4 + d][48 * j : 48 * j + 48, :] = refs[j][pl.ds(start, 48), :]


def combine_kernel(at_ref, ma_ref, mb_ref, s_ref, h_ref, l_ref, ga_ref, gb_ref, r0, r1, r2, r3, pa_ref, pb_ref, ta_ref, tb_ref, acc_ref):
    acc_ref[...] = jnp.zeros_like(acc_ref)

    def part(c):
        totals = [jnp.zeros((128, 512), jnp.float32)] * 2
        for d, r_ref in enumerate((r0, r1, r2, r3)):
            rows = r_ref[:, c]
            here = slice(192 * d, 192 * d + 192)
            for b, g_ref in enumerate((ga_ref, gb_ref)):
                lanes = slice(128 * b, 128 * b + 128)
                totals[b] = totals[b] + (dot(h_ref[here, lanes], rows, 0, 0) + dot(l_ref[here, lanes], rows, 0, 0))
                acc_ref[here, lanes] += dot(rows, g_ref[:, c], 1, 1)
        pa_ref[:, c] = totals[0].astype(jnp.bfloat16)
        pb_ref[:, c] = totals[1].astype(jnp.bfloat16)

    over_columns(4, 512, part)
    expert = plane_expert(at_ref, (768, 128), True).astype(jnp.float32)
    for b, (m_ref, t_ref) in enumerate(((ma_ref, ta_ref), (mb_ref, tb_ref))):
        lanes = slice(128 * b, 128 * b + 128)
        kept = jnp.where(s_ref[:, lanes] > 0.5, acc_ref[:, lanes], 0.0)
        for k in range(4):
            named = expert == m_ref[k : k + 1, :]
            t_ref[k : k + 1, :] = jnp.sum(jnp.where(named, kept, 0.0), axis=0, keepdims=True)
        t_ref[4:8, :] = jnp.zeros((4, 128), jnp.float32)


def gather_sum_kernel(s_ref, r0, r1, r2, r3, pa_ref, pb_ref):
    def part(c):
        for b, p_ref in enumerate((pa_ref, pb_ref)):
            total = jnp.zeros((128, 512), jnp.float32)
            for d, r_ref in enumerate((r0, r1, r2, r3)):
                total = total + dot(s_ref[192 * d : 192 * d + 192, 128 * b : 128 * b + 128], r_ref[:, c], 0, 0)
            p_ref[:, c] = total.astype(jnp.bfloat16)

    over_columns(4, 512, part)


def layer_call(kernel, out_shapes, at, args, weights, flops):
    steps, width = 4, 512

    def layer(w):
        if len(w.shape) == 2:
            return columns(w)
        if w.shape[3] == 2048:
            return pl.BlockSpec((1, 1, w.shape[2], width), lambda i, at: (at[0], 0, 0, i))
        return pl.BlockSpec((1, 1, width, w.shape[3]), lambda i, at: (at[0], 0, i, 0))

    whole = lambda a: pl.BlockSpec(a.shape, lambda i, at: (0, 0))
    columns = lambda a: pl.BlockSpec((a.shape[0], width), lambda i, at: (0, i))
    moved = sum(a.size * 2 for a in args) + sum(w.size for w in weights) + sum(s.size * 2 for s in out_shapes)
    return pl.pallas_call(
        kernel,
        out_shape=out_shapes,
        grid_spec=pltpu.PrefetchScalarGridSpec(
            num_scalar_prefetch=1,
            grid=(steps,),
            in_specs=[whole(a) for a in args] + [layer(w) for w in weights],
            out_specs=[columns(o) for o in out_shapes],
        ),
        compiler_params=pltpu.CompilerParams(vmem_limit_bytes=VMEM_LIMIT),
        cost_estimate=pl.CostEstimate(flops=flops, bytes_accessed=moved, transcendentals=0),
    )(at, *args, *weights)


def exchange(rows):
    return lax.all_to_all(rows.reshape(32, 24, 2048), SOURCE, 0, 0, tiled=True).reshape(768, 2048)


def step(tokens, expert_ids, route_weights, out_grad, gate_proj, up_proj, down_proj):
    f32, bf16 = jnp.float32, jnp.bfloat16
    sds = jax.ShapeDtypeStruct
    zh = lax.axis_index("zh")
    core = lax.axis_index("c")
    at = jnp.stack([lax.axis_index(name) for name in AXES])
    meta = jnp.concatenate([expert_ids[0].T.astype(f32), route_weights[0].T], axis=0)

    select = sds((768, 128), bf16)
    wide = sds((768, 256), bf16)
    rows_shape = sds((768, 2048), bf16)
    quarter = [sds((192, 2048), bf16)] * 4
    block_shape = sds((128, 2048), bf16)
    tiny = sds((8, 128), f32)
    own_meta = meta
    other_meta = move(own_meta, SWAP)
    other_tok = move(tokens[0], SWAP)
    other_og = move(out_grad[0], SWAP)
    near_meta = move(own_meta, CROSS)
    near_og = move(out_grad[0], CROSS)
    meta, pick, high, low = call(route_kernel, (tiny, select, select, select), [at], [own_meta, other_meta], 30_000_000)
    rows = call(pick_kernel, rows_shape, [at], [pick, tokens[0], other_tok], 400_000_000)
    rows = exchange(rows)
    grads, og = call(
        pick_weighted_kernel, (rows_shape, block_shape), [at], [high, low, out_grad[0], other_og], 800_000_000
    )
    grads = exchange(grads)
    back_pick, back_high, back_low, in_pick = call(back_route_kernel, (wide,) * 4, [at], [meta, near_meta], 120_000_000)

    w_gate = lax.dynamic_index_in_dim(gate_proj, zh, 0, keepdims=False)[0]
    w_up = lax.dynamic_index_in_dim(up_proj, zh, 0, keepdims=False)[0]
    w_down = lax.dynamic_index_in_dim(down_proj, zh, 0, keepdims=False)[0]
    gate_pre = dot(rows, w_gate, 1, 0)
    up_pre = dot(rows, w_up, 1, 0)
    sig = jax.nn.sigmoid(gate_pre)
    hidden = (gate_pre * sig * up_pre).astype(bf16)
    gate_pre, up_pre, hidden = lax.optimization_barrier((gate_pre, up_pre, hidden))

    def by_plane(value):
        return value.reshape(2, 16, 24, 768).transpose(1, 0, 2, 3).reshape(768, 768)

    turned = layer_call(turn_kernel, [sds((768, 2048), bf16)] * 2, at, [], [gate_proj, up_proj], 1000)
    outs = layer_call(down_kernel, quarter, at, [by_plane(hidden)], [down_proj], 2_400_000_000)
    outs = [outs[0]] + [move(outs[d], plane(-d, 0)) for d in (1, 3, 2)]
    outs = [outs[0], outs[1], outs[3], outs[2]]
    outs = call(functools.partial(regroup_kernel, 4), quarter, [at], outs, 1000)
    outs = [outs[0]] + [move(outs[d], plane(0, -d)) for d in (1, 2, 3)]
    part, far_part, gg, far_gg = call(
        combine_kernel,
        (block_shape, block_shape, tiny, tiny),
        [at],
        [meta, near_meta, back_pick, back_high, back_low, og, near_og] + outs,
        2_400_000_000,
        [pltpu.VMEM((768, 256), jnp.float32)],
    )

    def home(value):
        return jnp.where(core == 0, value, move(value, SWAP))

    def join(mine, far):
        far = move(far, CROSS)
        return (home(mine).astype(f32) + far.astype(f32)).astype(mine.dtype)

    layer_out = join(part, far_part)
    gate_grad = join(gg, far_gg)

    hidden_grad = dot(grads, w_down, 1, 1)
    sig = jax.nn.sigmoid(gate_pre)
    d_gate = (hidden_grad * up_pre * sig * (1.0 + gate_pre * (1.0 - sig))).astype(bf16)
    d_up = (hidden_grad * gate_pre * sig).astype(bf16)
    ins = layer_call(row_kernel, quarter, at, [by_plane(d_gate), by_plane(d_up)], turned, 4_800_000_000)
    ins = [ins[0]] + [move(ins[d], plane(0, -d)) for d in (1, 2, 3)]
    ins = call(functools.partial(regroup_kernel, 3), quarter, [at], ins, 1000)
    ins = [ins[0]] + [move(ins[d], plane(-d, 0)) for d in (1, 2, 3)]
    in_part, far_in = call(gather_sum_kernel, (block_shape, block_shape), [], [in_pick] + ins, 800_000_000)
    input_grad = join(in_part, far_in)

    mine = jnp.where(core == 0, zh, 1 - zh) * 384

    def down_grad(start):
        return dot(lax.dynamic_slice_in_dim(hidden, start, 384, 1), grads, 0, 0).astype(bf16)

    def gate_up_grad(start):
        cut = lambda v: lax.dynamic_slice_in_dim(v, start, 384, 1)
        return dot(rows, jnp.concatenate([cut(d_gate), cut(d_up)], axis=1), 0, 0).astype(bf16)

    def add(a, b):
        return (a.astype(f32) + b.astype(f32)).astype(bf16)

    down_there = move(down_grad(384 - mine), SIBLING)
    down_sum = add(down_grad(mine), down_there)
    down = home(down_sum)
    both_there = move(gate_up_grad(384 - mine), SIBLING)
    both_sum = add(gate_up_grad(mine), both_there)
    both = home(both_sum)
    layer_out = layer_out[None]
    input_grad = input_grad[None]
    gate_grad = gate_grad[:4].T[None]
    grad_gate, grad_up = both[None, None, :, :384], both[None, None, :, 384:]
    grad_down = down[None, None]
    return layer_out, input_grad, gate_grad, grad_gate, grad_up, grad_down


def solution(mesh):
    fine = Mesh(mesh.devices.reshape(SIZES), AXES)
    pipe, expert = ("zh", "c"), ("zl", "y", "x")
    tok = P(pipe, expert, None)
    weight = P(None, expert, None, None)
    grad = P(pipe, expert, None, None)
    return jax.shard_map(
        step,
        mesh=fine,
        in_specs=(tok, tok, tok, tok, weight, weight, weight),
        out_specs=(tok, tok, tok, grad, grad, grad),
        check_vma=False,
    )
```
